32 devices in a mesh: ctx: 4 (over y, core), head: 4 (over z), wide: 2 (over x).
Axes of the slice: x: 2, y: 2, z: 4, core: 2. Of those that a mesh axis runs over, the one named last changes fastest.
Arguments:
- query_rows: bfloat16 [2, 1024, 1024], P('wide', 'ctx', 'head'), may hold values from -105 to 105
- key_rows: bfloat16 [2, 1024, 1024], P('wide', 'ctx', 'head'), may hold values from -4.5 to 4.5
- value_rows: bfloat16 [2, 1024, 1024], P('wide', 'ctx', 'head'), may hold values from -6 to 6
- grad_out: bfloat16 [2, 1024, 1024], P('wide', 'ctx', 'head'), may hold values from -6 to 6
- segment: int32 [2, 1024], P('wide', 'ctx'), may hold values from 0 to 7, never falling along the last dimension, each value on 1 to 256 neighbouring positions
- frames: bfloat16 [2, 1024, 4096], P(None, 'ctx', 'wide'), may hold values from -6 to 6
Outputs:
- grad_query: bfloat16 [2, 1024, 1024], P('wide', 'ctx', 'head')
- grad_key: bfloat16 [2, 1024, 1024], P('wide', 'ctx', 'head')
- grad_value: bfloat16 [2, 1024, 1024], P('wide', 'ctx', 'head')
- grad_wq: float32 [2, 2048, 1024], P('wide', 'ctx', 'head')
The draws below stay inside these ranges and needn't reach their ends.
Inputs may be any that keep to these rules, and one draw needn't show every extreme that they name: Ids never fall along a recording; each segment spans 1 to 256 frames and one spans exactly 256.
All inputs are finite; a program needn't handle non-finite values.
Results may differ from the reference program's by a relative error of at most 0.01.
Values may be sent and summed in bfloat16 or wider, within the bound.
No kernel may reach another device: no remote copies, remote signals or barrier semaphores. Data moves between devices by JAX's collectives and lax.ppermute only.
A program may use at most 64 MiB of HBM per device.

```python
import math
import jax
import jax.numpy as jnp
import numpy as np
from jax import lax

D = 4096
HD = 128
TOK = 256
HEADS = 8
HQ = 1024
SEQ = 1024
RECS = 2
SEGMENTS = 8
N_WIDE = 2


def base_keys(key):
    return jnp.clip(jax.random.normal(jax.random.fold_in(key, 101), (RECS, SEQ, HQ), jnp.float32), -4.0, 4.0)


def draw_key_rows(key, part):
    base = base_keys(key)
    return base.astype(jnp.bfloat16)


def draw_query_rows(key, part):
    fresh = jnp.clip(jax.random.normal(jax.random.fold_in(key, 103), (RECS, SEQ, HQ), jnp.float32), -4.0, 4.0)
    return fresh.astype(jnp.bfloat16)


def with_spikes(values, key, source, target, shards_of, factor):
    def block_of(position):
        return (jnp.arange(values.shape[position]) // (values.shape[position] // shards_of)).reshape((-1,) + (1,) * (values.ndim - 1 - position))

    one_side = jax.random.permutation(key, shards_of)[block_of(target)]
    far = (block_of(target) + shards_of // 2) % shards_of
    return jnp.where((block_of(source) == one_side) | (block_of(source) == far), factor * values, values)


def level_of(key, shape, shards, least, largest):
    gain = 1.0
    for position, shards_of in shards:
        draws = jax.random.uniform(jax.random.fold_in(jax.random.fold_in(key, 6), position), (shards_of,), jnp.float32, least / len(shards), largest / len(shards))
        gain = gain * jnp.repeat(jnp.exp(draws), shape[position] // shards_of).reshape((-1,) + (1,) * (len(shape) - 1 - position))
    return gain


def profile(number_of, total, most, lean):
    weights = [(1 << 20) // math.isqrt(rank ** lean) + 1 for rank in range(2, number_of + 1)]
    rest, holding = total - most - (number_of - 1), [1] * (number_of - 1)
    while rest > 0:
        movable = [i for i in range(number_of - 1) if holding[i] < most]
        whole, budget = sum([weights[i] for i in movable]), rest
        for i in movable:
            addition = min(most - holding[i], max(1, budget * weights[i] // whole), rest)
            holding[i] = holding[i] + addition
            rest = rest - addition
    return np.array([most] + holding)


def uneven(stream_key, number_of, total, limit, lean):
    if number_of == 2:
        one = jax.random.randint(stream_key, (), max(1, total - limit), min(limit, total - 1) + 1)
        return jnp.stack([one, total - one])
    lengths = jnp.asarray(profile(number_of, total, limit, lean), jnp.int32)
    pairs = (number_of - 1) // 2
    donor, taker = lengths[1:1 + 2 * pairs:2], lengths[2:2 + 2 * pairs:2]
    margin = jnp.minimum(donor - 1, limit - taker)
    moved = jax.random.randint(jax.random.fold_in(stream_key, 1), (pairs,), 0, 1 << 20) % (margin + 1)
    lengths = lengths.at[1:1 + 2 * pairs:2].set(donor - moved).at[2:2 + 2 * pairs:2].set(taker + moved)
    return lengths[jax.random.permutation(jax.random.fold_in(stream_key, 2), number_of)]


def gaussian(key, extent, deviation, bound, shards=(), held_as=jnp.bfloat16):
    drawn = deviation * jax.random.normal(key, extent, jnp.float32)
    if shards:
        drawn = drawn * level_of(key, extent, shards, -0.22, 0.18)
    return jnp.clip(drawn, -bound, bound).astype(held_as)


def heavy_noise(key, extent, spread, bound, pieces, heavy, held_as=jnp.bfloat16):
    values = spread * jax.random.normal(key, extent, jnp.float32)
    if pieces:
        values = values * level_of(key, extent, pieces, -0.22, 0.18)
    return jnp.clip(with_spikes(values, jax.random.fold_in(key, 3), *heavy), -bound, bound).astype(held_as)


def setup_inputs(seed: int = 0) -> dict:
    splits = jax.random.split(jax.random.key(seed), 7)
    return {
        "query_rows": draw_query_rows(jax.random.fold_in(splits[6], 71), 0),
        "key_rows": draw_key_rows(jax.random.fold_in(splits[6], 71), 0),
        "value_rows": gaussian(splits[2], (RECS, SEQ, HQ), 1.0, 6.0, ((0, 2), (1, 4), (2, 4))),
        "grad_out": gaussian(splits[3], (RECS, SEQ, HQ), 1.0, 6.0, ((0, 2), (1, 4), (2, 4))),
        "segment": jax.vmap(lambda own: jnp.searchsorted(jnp.cumsum(uneven(own, SEGMENTS, SEQ, TOK, 1)), jnp.arange(SEQ), side="right"))(jax.random.split(splits[4], RECS)).reshape((RECS, SEQ)).astype(jnp.int32),
        "frames": heavy_noise(splits[5], (RECS, SEQ, D), 1.0, 6.0, ((1, 4), (2, 2)), (1, 2, 4, 2.0)),
    }


def windows(blocks, filler):
    earlier = jnp.concatenate([filler, blocks[:-1]], axis=0)
    return jnp.concatenate([earlier, blocks], axis=1)


def head_grads(inputs):
    query_head, key_head, value_head, grad_head, segment_head = inputs
    blocks = SEQ // TOK
    factor = HD ** -0.5
    query_block = query_head.reshape(blocks, TOK, HD).astype(jnp.float32)
    grad_block = grad_head.reshape(blocks, TOK, HD).astype(jnp.float32)
    key_window = windows(key_head.reshape(blocks, TOK, HD), jnp.zeros((1, TOK, HD), key_head.dtype)).astype(jnp.float32)
    value_window = windows(value_head.reshape(blocks, TOK, HD), jnp.zeros((1, TOK, HD), value_head.dtype)).astype(jnp.float32)
    segment_block = segment_head.reshape(blocks, TOK)
    segment_window = windows(segment_block, jnp.full((1, TOK), -1, jnp.int32))
    places = jnp.arange(TOK, dtype=jnp.int32)
    key_places = jnp.concatenate([places - TOK, places])
    allowed = (segment_block[:, :, None] == segment_window[:, None, :]) & (key_places[None, None, :] <= places[None, :, None])
    scores = jnp.einsum("bid,bjd->bij", query_block, key_window) * factor
    row_max = jnp.max(jnp.where(allowed, scores, -jnp.inf), axis=2, keepdims=True)
    row_total = jnp.sum(jnp.where(allowed, jnp.exp(scores - row_max), 0.0), axis=2, keepdims=True)
    log_total = row_max + jnp.log(row_total)
    prob = jnp.where(allowed, jnp.exp(scores - log_total), 0.0)
    prob_low = prob.astype(jnp.bfloat16)
    grad_prob = jnp.einsum("bid,bjd->bij", grad_block, value_window)
    row_delta = jnp.sum(prob * grad_prob, axis=2, keepdims=True)
    grad_score = (prob * (grad_prob - row_delta)).astype(jnp.bfloat16).astype(jnp.float32)
    grad_query = (jnp.einsum("bij,bjd->bid", grad_score, key_window) * factor).astype(jnp.bfloat16)
    key_window_grad = jnp.einsum("bij,bid->bjd", grad_score, query_block)
    value_window_grad = jnp.einsum("bij,bid->bjd", prob_low.astype(jnp.float32), grad_block)
    zero_block = jnp.zeros((1, TOK, HD), jnp.float32)
    key_grad = (key_window_grad[:, TOK:] + jnp.concatenate([key_window_grad[1:, :TOK], zero_block], axis=0)) * factor
    value_grad = value_window_grad[:, TOK:] + jnp.concatenate([value_window_grad[1:, :TOK], zero_block], axis=0)
    return (grad_query.reshape(SEQ, HD), key_grad.astype(jnp.bfloat16).reshape(SEQ, HD),
            value_grad.astype(jnp.bfloat16).reshape(SEQ, HD))


def to_heads(array):
    return array.reshape(RECS, SEQ, HEADS, HD).transpose(0, 2, 1, 3).reshape(RECS * HEADS, SEQ, HD)


def from_heads(array):
    return array.reshape(RECS, HEADS, SEQ, HD).transpose(0, 2, 1, 3).reshape(RECS, SEQ, HEADS * HD)


def reference(query_rows, key_rows, value_rows, grad_out, segment, frames):
    segment_all = jnp.repeat(segment, HEADS, axis=0)
    grad_query, grad_key, grad_value = lax.map(head_grads, (to_heads(query_rows), to_heads(key_rows), to_heads(value_rows), to_heads(grad_out), segment_all))
    grad_query = from_heads(grad_query)
    grad_wq = jnp.dot(frames.reshape(RECS * SEQ, D).T, grad_query.reshape(RECS * SEQ, HQ), preferred_element_type=jnp.float32)
    return grad_query, from_heads(grad_key), from_heads(grad_value), grad_wq.reshape(N_WIDE, D // N_WIDE, HQ)
```

```python
import functools

import jax
import jax.numpy as jnp
from jax import lax
from jax.experimental import pallas as pl
from jax.experimental.pallas import tpu as pltpu
from jax.sharding import PartitionSpec as P

HD = 128
F32 = jnp.float32
BF16 = jnp.bfloat16


def dot(left, right, left_dim, right_dim):
    return lax.dot_general(
        left, right, (((left_dim,), (right_dim,)), ((), ())), preferred_element_type=F32
    )


def call(body, outs, *args, flops=1 << 20, name=None):
    whole = pl.BlockSpec(memory_space=pltpu.VMEM)
    size = sum(a.size * a.dtype.itemsize for a in args)
    return pl.pallas_call(
        body,
        out_shape=outs,
        in_specs=[whole] * len(args),
        out_specs=jax.tree.map(lambda _: whole, outs),
        cost_estimate=pl.CostEstimate(flops=flops, bytes_accessed=size, transcendentals=0),
        name=name,
    )(*args)


def shape(dims, dtype):
    return jax.ShapeDtypeStruct(dims, dtype)


def spread(row, length):
    part = jnp.transpose(jnp.broadcast_to(row.astype(F32), (HD, length)))
    return jnp.concatenate([part] * (length // HD), axis=1)


def lower(length):
    rows = lax.broadcasted_iota(jnp.int32, (length, length), 0)
    columns = lax.broadcasted_iota(jnp.int32, (length, length), 1)
    return rows, columns


def scores_body(length, heads, q, k, v, g, pk, pv, seg, pseg, dq, ds_out, p_out):
    factor = HD ** (-0.5)
    key_place, query_place = lower(length)
    own = key_place <= query_place
    seg_row = seg[...].astype(F32)
    seg_column = jnp.where(own, spread(seg[...], length), spread(pseg[...], length))
    valid = seg_column == seg_row
    for h in range(heads):
        at = slice(h * HD, (h + 1) * HD)
        qh, gh, kh, pkh = q[:, at], g[:, at], k[:, at], pk[:, at]
        scores = jnp.where(own, dot(kh, qh, 1, 1), dot(pkh, qh, 1, 1)) * factor
        scores = jnp.where(valid, scores, -jnp.inf)
        top = jnp.max(scores, axis=0, keepdims=True)
        weight = jnp.exp(scores - top)
        prob = weight * (1.0 / jnp.sum(weight, axis=0, keepdims=True))
        grad_prob = jnp.where(own, dot(v[:, at], gh, 1, 1), dot(pv[:, at], gh, 1, 1))
        delta = jnp.sum(prob * grad_prob, axis=0, keepdims=True)
        grad_score = prob * (grad_prob - delta)
        own_part = jnp.where(own, grad_score, 0.0).astype(BF16)
        prior_part = jnp.where(own, 0.0, grad_score).astype(BF16)
        dq[:, at] = (
            (dot(own_part, kh, 0, 0) + dot(prior_part, pkh, 0, 0)) * factor
        ).astype(BF16)
        ds_out[h] = grad_score.astype(BF16)
        p_out[h] = prob.astype(BF16)


def terms_body(length, heads, q, g, ds, p, own_out, back_out):
    key_place, query_place = lower(length)
    own = key_place <= query_place
    for h in range(heads):
        at = slice(h * HD, (h + 1) * HD)
        for index, (left, right) in enumerate(((ds, q), (p, g))):
            value = left[h].astype(F32)
            own_out[index, :, at] = dot(
                jnp.where(own, value, 0.0).astype(BF16), right[:, at], 1, 0
            )
            back_out[index, :, at] = dot(
                jnp.where(own, 0.0, value).astype(BF16), right[:, at], 1, 0
            ).astype(BF16)


def join_body(own, later, dk, dv):
    dk[...] = ((own[0] + later[0].astype(F32)) * HD ** (-0.5)).astype(BF16)
    dv[...] = (own[1] + later[1].astype(F32)).astype(BF16)


def turn_body(recs, length, block, parts, frames, mine, theirs):
    for side in range(2):

        @pl.when(lax.rem(lax.axis_index("ctx"), 2) == side)
        def _():
            for part in range(parts):
                for r in range(recs):
                    for out, which in ((mine, side), (theirs, 1 - side)):
                        start = (2 * part + which) * block
                        tile = frames[r, :, start : start + block]
                        out[part, :, r * length : (r + 1) * length] = jnp.transpose(tile)


def panel_body(count, length, block, step, *refs):
    frames, grads, out = refs[:2], refs[2:-1], refs[-1]
    part = lax.rem(lax.div(lax.axis_index("ctx"), 2) + step, lax.axis_size("ctx") // 2)
    wide = lax.axis_index("wide")
    total = None
    for k in range(count):
        rec = lax.rem(wide - k + count, count)
        at = pl.ds(pl.multiple_of(rec * length, HD), length)
        for core in range(2):
            term = dot(frames[core][part, :, at], grads[2 * k + core][...], 1, 0)
            total = term if total is None else total + term
    out[...] = total.astype(out.dtype)


def add_body(*refs):
    total = refs[0][...]
    for ref in refs[1:-1]:
        total = total + ref[...].astype(F32)
    refs[-1][...] = total


def shards(query_rows, key_rows, value_rows, grad_out, segment, frames):
    length, columns = query_rows.shape[1:]
    heads = columns // HD
    ctx_count = lax.axis_size("ctx")
    wide_count = lax.axis_size("wide")
    recs, _, width = frames.shape
    block = width // ctx_count
    parts = ctx_count // 2
    assert ctx_count >= 4 and recs == wide_count
    onward = [(i, (i + 1) % ctx_count) for i in range(ctx_count)]
    back = [(i, (i - 1) % ctx_count) for i in range(ctx_count)]
    other = [(i, i ^ 1) for i in range(ctx_count)]

    q, k, v, g = (a[0] for a in (query_rows, key_rows, value_rows, grad_out))
    pseg = lax.ppermute(segment, "ctx", onward)
    pk = lax.ppermute(k, "ctx", onward)
    pv = lax.ppermute(v, "ctx", onward)

    turned = shape((parts, block, recs * length), BF16)
    mine, theirs = call(
        functools.partial(turn_body, recs, length, block, parts), (turned, turned), frames, name="turn"
    )
    given = lax.ppermute(theirs, "ctx", other)

    square = shape((heads, length, length), BF16)
    dq, ds, p = call(
        functools.partial(scores_body, length, heads),
        (shape((length, columns), BF16), square, square),
        q, k, v, g, pk, pv, segment, pseg, name="scores",
    )
    grads = []
    for step in range(wide_count):
        ring = [(i, (i + step) % wide_count) for i in range(wide_count)]
        piece = lax.ppermute(dq, "wide", ring) if step else dq
        grads += [piece, lax.ppermute(piece, "ctx", other)]

    own, to_prior = call(
        functools.partial(terms_body, length, heads),
        (shape((2, length, columns), F32), shape((2, length, columns), BF16)),
        q, g, ds, p, name="terms",
    )
    later = lax.ppermute(to_prior, "ctx", back)

    def panel(step):
        return call(
            functools.partial(panel_body, wide_count, length, block, step),
            shape((block, columns), BF16 if step else F32),
            mine, given, *grads, name="panel" + str(step),
        )

    arrived = []
    for step in range(1, parts):
        ring = [(i, (i + 2 * step) % ctx_count) for i in range(ctx_count)]
        arrived.append(lax.ppermute(panel(step), "ctx", ring))
    dk, dv = call(join_body, (shape((length, columns), BF16),) * 2, own, later, name="join")
    grad_wq = call(add_body, shape((block, columns), F32), panel(0), *arrived, name="add")
    return (dq[None], dk[None], dv[None], grad_wq[None])


def solution(mesh):
    rows = P("wide", "ctx", "head")
    return jax.shard_map(
        shards,
        mesh=mesh,
        in_specs=(rows, rows, rows, rows, P("wide", "ctx"), P(None, "ctx", "wide")),
        out_specs=(rows, rows, rows, rows),
        check_vma=False,
    )
```

```python
import functools

import jax
import jax.numpy as jnp
from jax import lax
from jax.experimental import pallas as pl
from jax.experimental.pallas import tpu as pltpu
from jax.sharding import PartitionSpec as P


HD = 128
F32 = jnp.float32
BF16 = jnp.bfloat16


def dot(left, right, left_dim, right_dim):
    return lax.dot_general(
        left, right, (((left_dim,), (right_dim,)), ((), ())), preferred_element_type=F32
    )


def vmem(dims, dtype):
    return pltpu.VMEM(dims, dtype)


def call(body, outs, *args, cost=1):
    whole = pl.BlockSpec(memory_space=pltpu.VMEM)
    args = [pltpu.with_memory_space_constraint(a, pltpu.VMEM) for a in args]
    return pl.pallas_call(
        body,
        out_shape=outs,
        in_specs=[whole] * len(args),
        out_specs=jax.tree.map(lambda _: whole, outs, is_leaf=lambda o: not isinstance(o, tuple)),
        cost_estimate=pl.CostEstimate(flops=cost << 20, bytes_accessed=1 << 20, transcendentals=0),
        compiler_params=pltpu.CompilerParams(vmem_limit_bytes=24 << 20),
    )(*args)


def shape(dims, dtype):
    return jax.ShapeDtypeStruct(dims, dtype)


def spread(row, length):
    part = jnp.transpose(jnp.broadcast_to(row.astype(F32), (HD, length)))
    return jnp.concatenate([part] * (length // HD), axis=1)


def lower(length):
    rows = lax.broadcasted_iota(jnp.int32, (length, length), 0)
    columns = lax.broadcasted_iota(jnp.int32, (length, length), 1)
    return rows, columns


def scores_body(length, heads, q, k, v, g, pk, pv, seg, pseg, dq, ds_out, p_out):
    factor = HD ** (-0.5)
    key_place, query_place = lower(length)
    own = key_place <= query_place
    seg_row = seg[...].astype(F32)
    seg_column = jnp.where(own, spread(seg[...], length), spread(pseg[...], length))
    valid = seg_column == seg_row
    for h in range(heads):
        at = slice(h * HD, (h + 1) * HD)
        qh, gh, kh, pkh = q[:, at], g[:, at], k[:, at], pk[:, at]
        scores = jnp.where(own, dot(kh, qh, 1, 1), dot(pkh, qh, 1, 1)) * factor
        scores = jnp.where(valid, scores, -jnp.inf)
        top = jnp.max(scores, axis=0, keepdims=True)
        weight = jnp.exp(scores - top)
        prob = weight * (1.0 / jnp.sum(weight, axis=0, keepdims=True))
        grad_prob = jnp.where(own, dot(v[:, at], gh, 1, 1), dot(pv[:, at], gh, 1, 1))
        delta = jnp.sum(prob * grad_prob, axis=0, keepdims=True)
        grad_score = prob * (grad_prob - delta)
        own_part = jnp.where(own, grad_score, 0.0).astype(BF16)
        prior_part = jnp.where(own, 0.0, grad_score).astype(BF16)
        dq[:, at] = (
            (dot(own_part, kh, 0, 0) + dot(prior_part, pkh, 0, 0)) * factor
        ).astype(BF16)
        ds_out[h] = grad_score.astype(BF16)
        p_out[h] = prob.astype(BF16)


def terms_body(length, heads, q, g, ds, p, own_out, back_out):
    key_place, query_place = lower(length)
    own = key_place <= query_place
    for h in range(heads):
        at = slice(h * HD, (h + 1) * HD)
        for index, (left, right) in enumerate(((ds, q), (p, g))):
            value = left[h].astype(F32)
            own_out[index, :, at] = dot(
                jnp.where(own, value, 0.0).astype(BF16), right[:, at], 1, 0
            )
            back_out[index, :, at] = dot(
                jnp.where(own, 0.0, value).astype(BF16), right[:, at], 1, 0
            ).astype(BF16)


def join_body(own, later, dk, dv):
    dk[...] = ((own[0] + later[0].astype(F32)) * HD ** (-0.5)).astype(BF16)
    dv[...] = (own[1] + later[1].astype(F32)).astype(BF16)


def turn_body(recs, length, block, parts, frames, mine, theirs):
    for side in range(2):

        @pl.when(lax.rem(lax.axis_index("ctx"), 2) == side)
        def _():
            for part in range(parts):
                for r in range(recs):
                    for out, which in ((mine, side), (theirs, 1 - side)):
                        start = (2 * part + which) * block
                        tile = frames[r, :, start : start + block]
                        out[part, :, r * length : (r + 1) * length] = jnp.transpose(tile)


def panel_body(count, length, step, *refs):
    frames, grads, out = refs[:2], refs[2:-1], refs[-1]
    part = lax.rem(lax.div(lax.axis_index("ctx"), 2) + step, lax.axis_size("ctx") // 2)
    wide = lax.axis_index("wide")
    total = None
    for k in range(count):
        rec = lax.rem(wide - k + count, count)
        at = pl.ds(pl.multiple_of(rec * length, HD), length)
        for core in range(2):
            term = dot(frames[core][part, :, at], grads[2 * k + core][...], 1, 0)
            total = term if total is None else total + term
    out[...] = total.astype(out.dtype)


def add_body(*refs):
    total = refs[0][...]
    for ref in refs[1:-1]:
        total = total + ref[...].astype(F32)
    refs[-1][...] = total


def shards(query_rows, key_rows, value_rows, grad_out, segment, frames):
    length, columns = query_rows.shape[1:]
    heads = columns // HD
    ctx_count = lax.axis_size("ctx")
    wide_count = lax.axis_size("wide")
    recs, _, width = frames.shape
    block = width // ctx_count
    parts = ctx_count // 2
    assert ctx_count >= 4 and recs == wide_count
    onward = [(i, (i + 1) % ctx_count) for i in range(ctx_count)]
    back = [(i, (i - 1) % ctx_count) for i in range(ctx_count)]
    other = [(i, i ^ 1) for i in range(ctx_count)]

    q, k, v, g = (a[0] for a in (query_rows, key_rows, value_rows, grad_out))
    pseg = lax.ppermute(segment, "ctx", onward)
    pk = lax.ppermute(k, "ctx", onward)
    pv = lax.ppermute(v, "ctx", onward)

    turned = vmem((parts, block, recs * length), BF16)
    mine, theirs = call(
        functools.partial(turn_body, recs, length, block, parts), (turned, turned), frames
    )
    given = lax.ppermute(theirs, "ctx", other)

    square = vmem((heads, length, length), BF16)
    dq, ds, p = call(
        functools.partial(scores_body, length, heads),
        (vmem((length, columns), BF16), square, square),
        q, k, v, g, pk, pv, segment, pseg,
    )
    grads = []
    for step in range(wide_count):
        ring = [(i, (i + step) % wide_count) for i in range(wide_count)]
        piece = dq
        if step:
            piece = lax.ppermute(dq, "wide", ring)
        grads += [piece, lax.ppermute(piece, "ctx", other)]

    own, to_prior = call(
        functools.partial(terms_body, length, heads),
        (vmem((2, length, columns), F32), vmem((2, length, columns), BF16)),
        q, g, ds, p,
    )
    later = lax.ppermute(to_prior, "ctx", back)

    def panel(step):
        return call(
            functools.partial(panel_body, wide_count, length, step),
            vmem((block, columns), BF16 if step else F32),
            mine, given, *grads,
        )

    arrived = []
    for step in range(1, parts):
        ring = [(i, (i + 2 * step) % ctx_count) for i in range(ctx_count)]
        piece = panel(step)
        arrived.append(lax.ppermute(piece, "ctx", ring))
    dk, dv = call(join_body, (shape((length, columns), BF16),) * 2, own, later)
    kept = panel(0)
    grad_wq = call(add_body, shape((block, columns), F32), kept, *arrived)
    return (dq[None], dk[None], dv[None], grad_wq[None])


def solution(mesh):
    rows = P("wide", "ctx", "head")
    return jax.shard_map(
        shards,
        mesh=mesh,
        in_specs=(rows, rows, rows, rows, P("wide", "ctx"), P(None, "ctx", "wide")),
        out_specs=(rows, rows, rows, rows),
        check_vma=False,
    )
```

```python
import functools

import jax
import jax.numpy as jnp
from jax import lax
from jax.experimental import pallas as pl
from jax.experimental.pallas import tpu as pltpu
from jax.sharding import PartitionSpec as P


CHUNKS = 2
HD = 128
F32 = jnp.float32
BF16 = jnp.bfloat16


def dot(left, right, left_dim, right_dim):
    return lax.dot_general(
        left, right, (((left_dim,), (right_dim,)), ((), ())), preferred_element_type=F32
    )


def vmem(dims, dtype):
    return pltpu.VMEM(dims, dtype)


def call(body, outs, *args, cost=1):
    whole = pl.BlockSpec(memory_space=pltpu.VMEM)
    args = [pltpu.with_memory_space_constraint(a, pltpu.VMEM) for a in args]
    return pl.pallas_call(
        body,
        out_shape=outs,
        in_specs=[whole] * len(args),
        out_specs=jax.tree.map(lambda _: whole, outs, is_leaf=lambda o: not isinstance(o, tuple)),
        cost_estimate=pl.CostEstimate(flops=cost << 20, bytes_accessed=1 << 20, transcendentals=0),
        compiler_params=pltpu.CompilerParams(vmem_limit_bytes=24 << 20),
    )(*args)


def shape(dims, dtype):
    return jax.ShapeDtypeStruct(dims, dtype)


def spread(row, length):
    part = jnp.transpose(jnp.broadcast_to(row.astype(F32), (HD, length)))
    return jnp.concatenate([part] * (length // HD), axis=1)


def lower(length):
    rows = lax.broadcasted_iota(jnp.int32, (length, length), 0)
    return rows <= lax.broadcasted_iota(jnp.int32, (length, length), 1)


def masks(length, seg, pseg):
    own = lower(length)
    column = jnp.where(own, spread(seg[...], length), spread(pseg[...], length))
    return own, column == seg[...].astype(F32)


def head_prob(own, valid, qh, kh, pkh):
    scores = jnp.where(own, dot(kh, qh, 1, 1), dot(pkh, qh, 1, 1)) * HD ** (-0.5)
    scores = jnp.where(valid, scores, -jnp.inf)
    top = jnp.max(scores, axis=0, keepdims=True)
    weight = jnp.exp(scores - top)
    return weight * (1.0 / jnp.sum(weight, axis=0, keepdims=True))


def prob_body(length, heads, q, k, v, g, pk, seg, pseg, prob, own_grad):
    own, valid = masks(length, seg, pseg)
    for h in range(heads):
        at = slice(h * HD, (h + 1) * HD)
        prob[h] = head_prob(own, valid, q[:, at], k[:, at], pk[:, at])
        own_grad[h] = dot(v[:, at], g[:, at], 1, 1)


def query_body(length, heads, k, g, pk, pv, prob, own_grad, dq, ds):
    own = lower(length)
    own_query = jnp.logical_not(own) | (
        lax.broadcasted_iota(jnp.int32, (length, length), 0)
        == lax.broadcasted_iota(jnp.int32, (length, length), 1)
    )
    for h in range(heads):
        at = slice(h * HD, (h + 1) * HD)
        grad_prob = jnp.where(own, own_grad[h], dot(pv[:, at], g[:, at], 1, 1))
        grad_score = prob[h] * (
            grad_prob - jnp.sum(prob[h] * grad_prob, axis=0, keepdims=True)
        )
        ds[h] = grad_score
        turned = jnp.transpose(grad_score)
        own_part = jnp.where(own_query, turned, 0.0).astype(BF16)
        prior_part = jnp.where(own_query, 0.0, turned).astype(BF16)
        total = dot(own_part, k[:, at], 1, 0) + dot(prior_part, pk[:, at], 1, 0)
        dq[:, at] = (total * HD ** (-0.5)).astype(BF16)


def terms_body(length, heads, q, g, prob, ds, own_out, back_out):
    own = lower(length)
    for h in range(heads):
        at = slice(h * HD, (h + 1) * HD)
        for index, (left, right) in enumerate(((ds[h], q), (prob[h], g))):
            own_out[index, :, at] = dot(
                jnp.where(own, left, 0.0).astype(BF16), right[:, at], 1, 0
            )
            back_out[index, :, at] = dot(
                jnp.where(own, 0.0, left).astype(BF16), right[:, at], 1, 0
            ).astype(BF16)


def join_body(own, later, dk, dv):
    dk[...] = ((own[0] + later[0].astype(F32)) * HD ** (-0.5)).astype(BF16)
    dv[...] = (own[1] + later[1].astype(F32)).astype(BF16)


def turn_body(recs, length, block, parts, frames, mine, theirs):
    for side in range(2):

        @pl.when(lax.rem(lax.axis_index("ctx"), 2) == side)
        def _():
            for part in range(parts):
                for r in range(recs):
                    for out, which in ((mine, side), (theirs, 1 - side)):
                        start = (2 * part + which) * block
                        tile = frames[r, :, start : start + block]
                        out[part, :, r * length : (r + 1) * length] = jnp.transpose(tile)


def panel_body(count, length, first, step, *refs):
    frames, grads, out = refs[:2], refs[2:-1], refs[-1]
    part = lax.rem(lax.div(lax.axis_index("ctx"), 2) + step, lax.axis_size("ctx") // 2)
    wide = lax.axis_index("wide")
    total = None
    for k in range(count):
        rec = lax.rem(wide - k + count, count)
        at = pl.ds(pl.multiple_of(rec * length, HD), length)
        for core in range(2):
            rows = frames[core][part, first : first + out.shape[0], at]
            term = dot(rows, grads[2 * k + core][...], 1, 0)
            total = term if total is None else total + term
    out[...] = total.astype(out.dtype)


def add_body(first, *refs):
    refs, out = (refs[:-1] if first == 0 else refs[:-2]), refs[-1]
    total = refs[0][first : first + out.shape[0]]
    for ref in refs[1:]:
        total = total + ref[...].astype(F32)
    out[...] = total


def add(first, kept, arrived, held):
    whole = pl.BlockSpec(memory_space=pltpu.VMEM)
    rows, columns = arrived[0].shape
    args = [pltpu.with_memory_space_constraint(a, pltpu.VMEM) for a in (kept, *arrived)]
    return pl.pallas_call(
        functools.partial(add_body, first),
        grid=(1,),
        out_shape=shape(kept.shape, F32),
        in_specs=[whole] * len(args) + [pl.BlockSpec(memory_space=pl.ANY)] * len(held),
        out_specs=pl.BlockSpec((rows, columns), lambda i: (first // rows, 0)),
        input_output_aliases={len(args): 0} if held else {},
        cost_estimate=pl.CostEstimate(flops=1 << 20, bytes_accessed=1 << 20, transcendentals=0),
        compiler_params=pltpu.CompilerParams(vmem_limit_bytes=24 << 20),
    )(*args, *held)


def shards(query_rows, key_rows, value_rows, grad_out, segment, frames):
    length, columns = query_rows.shape[1:]
    heads = columns // HD
    ctx_count = lax.axis_size("ctx")
    wide_count = lax.axis_size("wide")
    recs, _, width = frames.shape
    block = width // ctx_count
    parts = ctx_count // 2
    assert ctx_count >= 4 and recs == wide_count
    onward = [(i, (i + 1) % ctx_count) for i in range(ctx_count)]
    back = [(i, (i - 1) % ctx_count) for i in range(ctx_count)]
    other = [(i, i ^ 1) for i in range(ctx_count)]
    q, k, v, g = (a[0] for a in (query_rows, key_rows, value_rows, grad_out))

    def sent(value, pairs):
        return lax.ppermute(value, "ctx", pairs)

    pseg = sent(segment, onward)
    pk = sent(k, onward)
    pv = sent(v, onward)

    turned = vmem((parts, block, recs * length), BF16)
    mine, theirs = call(
        functools.partial(turn_body, recs, length, block, parts), (turned, turned), frames
    )
    given = lax.ppermute(theirs, "ctx", other)

    square = vmem((heads, length, length), F32)
    prob, own_grad = call(
        functools.partial(prob_body, length, heads), (square, square),
        q, k, v, g, pk, segment, pseg,
    )
    dq, ds = call(
        functools.partial(query_body, length, heads), (vmem((length, columns), BF16), square),
        k, g, pk, pv, prob, own_grad,
    )
    grads = []
    for step in range(wide_count):
        ring = [(i, (i + step) % wide_count) for i in range(wide_count)]
        piece = dq
        if step:
            piece = lax.ppermute(dq, "wide", ring)
        grads += [piece, sent(piece, other)]

    own, to_prior = call(
        functools.partial(terms_body, length, heads),
        (vmem((2, length, columns), F32), vmem((2, length, columns), BF16)),
        q, g, prob, ds,
    )
    later = sent(to_prior, back)

    def panel(first, rows, step, dtype):
        return call(
            functools.partial(panel_body, wide_count, length, first, step),
            vmem((rows, columns), dtype),
            mine, given, *grads,
        )

    chunks = CHUNKS
    rows = block // chunks
    arrived = [[] for _ in range(chunks)]
    for step in range(1, parts):
        ring = [(i, (i + 2 * step) % ctx_count) for i in range(ctx_count)]
        for c in range(chunks):
            piece = panel(c * rows, rows, step, BF16)
            arrived[c].append(sent(piece, ring))
    dk, dv = call(join_body, (shape((length, columns), BF16),) * 2, own, later)
    kept = panel(0, block, 0, F32)
    held = []
    for c in range(chunks):
        held = [add(c * rows, kept, arrived[c], held)]
    return (dq[None], dk[None], dv[None], held[0][None])


def solution(mesh):
    rows = P("wide", "ctx", "head")
    return jax.shard_map(
        shards,
        mesh=mesh,
        in_specs=(rows, rows, rows, rows, P("wide", "ctx"), P(None, "ctx", "wide")),
        out_specs=(rows, rows, rows, rows),
        check_vma=False,
    )
```

```python
import functools

import jax
import jax.numpy as jnp
from jax import lax
from jax.experimental import pallas as pl
from jax.experimental.pallas import tpu as pltpu
from jax.sharding import PartitionSpec as P


HD = 128
F32 = jnp.float32
BF16 = jnp.bfloat16


def dot(left, right, left_dim, right_dim):
    return lax.dot_general(
        left, right, (((left_dim,), (right_dim,)), ((), ())), preferred_element_type=F32
    )


def vmem(dims, dtype):
    return pltpu.VMEM(dims, dtype)


def call(body, outs, *args, cost=1):
    whole = pl.BlockSpec(memory_space=pltpu.VMEM)
    args = [pltpu.with_memory_space_constraint(a, pltpu.VMEM) for a in args]
    return pl.pallas_call(
        body,
        out_shape=outs,
        in_specs=[whole] * len(args),
        out_specs=jax.tree.map(lambda _: whole, outs, is_leaf=lambda o: not isinstance(o, tuple)),
        cost_estimate=pl.CostEstimate(flops=cost << 20, bytes_accessed=1 << 20, transcendentals=0),
        compiler_params=pltpu.CompilerParams(vmem_limit_bytes=24 << 20),
    )(*args)


def shape(dims, dtype):
    return jax.ShapeDtypeStruct(dims, dtype)


def spread(row, length):
    part = jnp.transpose(jnp.broadcast_to(row.astype(F32), (HD, length)))
    return jnp.concatenate([part] * (length // HD), axis=1)


def head(h):
    return slice(h * HD, (h + 1) * HD)


def lower(length):
    rows = lax.broadcasted_iota(jnp.int32, (length, length), 0)
    return rows <= lax.broadcasted_iota(jnp.int32, (length, length), 1)


def masks(length, seg, pseg):
    own = lower(length)
    column = jnp.where(own, spread(seg[...], length), spread(pseg[...], length))
    return own, column == seg[...].astype(F32)


def head_prob(own, valid, qh, kh, pkh):
    scores = jnp.where(own, dot(kh, qh, 1, 1), dot(pkh, qh, 1, 1)) * HD ** (-0.5)
    scores = jnp.where(valid, scores, -jnp.inf)
    top = jnp.max(scores, axis=0, keepdims=True)
    weight = jnp.exp(scores - top)
    return weight * (1.0 / jnp.sum(weight, axis=0, keepdims=True))


def prob_body(length, heads, q, k, v, g, pk, seg, pseg, prob, own_grad):
    own, valid = masks(length, seg, pseg)
    for h in range(heads):
        at = head(h)
        prob[h] = head_prob(own, valid, q[:, at], k[:, at], pk[:, at])
        own_grad[h] = dot(v[:, at], g[:, at], 1, 1)


def query_body(length, heads, first, k, g, pk, pv, prob, own_grad, dq, ds):
    own = lower(length)
    own_query = jnp.logical_not(own) | (
        lax.broadcasted_iota(jnp.int32, (length, length), 0)
        == lax.broadcasted_iota(jnp.int32, (length, length), 1)
    )
    for h in range(heads):
        at = head(first + h)
        weight = prob[first + h]
        grad_prob = jnp.where(own, own_grad[first + h], dot(pv[:, at], g[:, at], 1, 1))
        grad_score = weight * (
            grad_prob - jnp.sum(weight * grad_prob, axis=0, keepdims=True)
        )
        ds[h] = grad_score
        turned = jnp.transpose(grad_score)
        own_part = jnp.where(own_query, turned, 0.0).astype(BF16)
        prior_part = jnp.where(own_query, 0.0, turned).astype(BF16)
        total = dot(own_part, k[:, at], 1, 0) + dot(prior_part, pk[:, at], 1, 0)
        dq[:, head(h)] = (total * HD ** (-0.5)).astype(BF16)


def terms_body(length, heads, size, q, g, prob, *refs):
    own_out, back_out, dq_out = refs[-3:]
    pieces = [refs[i : i + 2] for i in range(0, len(refs) - 3, 2)]
    own = lower(length)
    for c, (dq, _) in enumerate(pieces):
        dq_out[:, c * size * HD : (c + 1) * size * HD] = dq[...]
    for h in range(heads):
        at = head(h)
        ds = pieces[h // size][1]
        for index, (left, right) in enumerate(((ds[h % size], q), (prob[h], g))):
            own_out[index, :, at] = dot(
                jnp.where(own, left, 0.0).astype(BF16), right[:, at], 1, 0
            )
            back_out[index, :, at] = dot(
                jnp.where(own, 0.0, left).astype(BF16), right[:, at], 1, 0
            ).astype(BF16)


def join_body(own, later, dk, dv):
    dk[...] = ((own[0] + later[0].astype(F32)) * HD ** (-0.5)).astype(BF16)
    dv[...] = (own[1] + later[1].astype(F32)).astype(BF16)


def turn_body(recs, length, block, parts, frames, mine, theirs):
    for side in range(2):

        @pl.when(lax.rem(lax.axis_index("ctx"), 2) == side)
        def _():
            for part in range(parts):
                for r in range(recs):
                    for out, which in ((mine, side), (theirs, 1 - side)):
                        start = (2 * part + which) * block
                        tile = frames[r, :, start : start + block]
                        out[part, :, r * length : (r + 1) * length] = jnp.transpose(tile)


def panel_body(count, length, step, first, frames0, frames1, mine, peer, *refs):
    grads, out = refs[:-1], refs[-1]
    part = lax.rem(lax.div(lax.axis_index("ctx"), 2) + step, lax.axis_size("ctx") // 2)
    wide = lax.axis_index("wide")
    width = grads[0].shape[1]
    for c in range(out.shape[1] // width):
        at = slice((first + c) * width, (first + c + 1) * width)
        pairs = [(mine[:, at], peer[:, at])]
        for k in range(count - 1):
            i = 2 * (c * (count - 1) + k)
            pairs.append((grads[i][...], grads[i + 1][...]))
        total = None
        for k, pair in enumerate(pairs):
            rec = lax.rem(wide - k + count, count)
            rows = pl.ds(pl.multiple_of(rec * length, HD), length)
            for frames, grad in zip((frames0, frames1), pair):
                term = dot(frames[part, :, rows], grad, 1, 0)
                total = term if total is None else total + term
        out[:, c * width : (c + 1) * width] = total.astype(out.dtype)


def add_body(first, *refs):
    refs, out = (refs[:-1] if first == 0 else refs[:-2]), refs[-1]
    total = refs[0][:, first : first + out.shape[1]]
    for ref in refs[1:]:
        total = total + ref[...].astype(F32)
    out[...] = total


def add(first, kept, arrived, held):
    whole = pl.BlockSpec(memory_space=pltpu.VMEM)
    rows, columns = arrived[0].shape
    args = [pltpu.with_memory_space_constraint(a, pltpu.VMEM) for a in (kept, *arrived)]
    return pl.pallas_call(
        functools.partial(add_body, first),
        grid=(1,),
        out_shape=shape(kept.shape, F32),
        in_specs=[whole] * len(args) + [pl.BlockSpec(memory_space=pl.ANY)] * len(held),
        out_specs=pl.BlockSpec((rows, columns), lambda i: (0, first // columns)),
        input_output_aliases={len(args): 0} if held else {},
        cost_estimate=pl.CostEstimate(flops=1 << 20, bytes_accessed=1 << 20, transcendentals=0),
        compiler_params=pltpu.CompilerParams(vmem_limit_bytes=24 << 20),
    )(*args, *held)


def shards(query_rows, key_rows, value_rows, grad_out, segment, frames):
    length, columns = query_rows.shape[1:]
    heads = columns // HD
    ctx_count = lax.axis_size("ctx")
    wide_count = lax.axis_size("wide")
    recs, _, width = frames.shape
    block = width // ctx_count
    parts = ctx_count // 2
    assert ctx_count >= 4 and recs == wide_count
    onward = [(i, (i + 1) % ctx_count) for i in range(ctx_count)]
    back = [(i, (i - 1) % ctx_count) for i in range(ctx_count)]
    other = [(i, i ^ 1) for i in range(ctx_count)]
    q, k, v, g = (a[0] for a in (query_rows, key_rows, value_rows, grad_out))

    def sent(value, pairs):
        return lax.ppermute(value, "ctx", pairs)

    pseg = sent(segment, onward)
    pk = sent(k, onward)
    pv = sent(v, onward)

    turned = vmem((parts, block, recs * length), BF16)
    mine, theirs = call(
        functools.partial(turn_body, recs, length, block, parts), (turned, turned), frames
    )
    given = lax.ppermute(theirs, "ctx", other)

    chunks = 2 if heads % 2 == 0 else 1
    size = heads // chunks
    square = vmem((heads, length, length), F32)
    prob, own_grad = call(
        functools.partial(prob_body, length, heads), (square, square),
        q, k, v, g, pk, segment, pseg,
    )
    found = []
    for c in range(chunks):
        found += call(
            functools.partial(query_body, length, size, c * size),
            (vmem((length, size * HD), BF16), vmem((size, length, length), F32)),
            k, g, pk, pv, prob, own_grad,
        )
    own, to_prior, dq = call(
        functools.partial(terms_body, length, heads, size),
        (
            vmem((2, length, columns), F32),
            vmem((2, length, columns), BF16),
            vmem((length, columns), BF16),
        ),
        q, g, prob, *found,
    )
    later = sent(to_prior, back)
    peer = sent(dq, other)
    grads = []
    for c in range(chunks):
        pieces = []
        for step in range(1, wide_count):
            ring = [(i, (i + step) % wide_count) for i in range(wide_count)]
            piece = lax.ppermute(found[2 * c], "wide", ring)
            pieces += [piece, sent(piece, other)]
        grads.append(pieces)

    def panel(step, first, pieces, width, dtype):
        return call(
            functools.partial(panel_body, wide_count, length, step, first),
            vmem((block, width), dtype),
            mine, given, dq, peer, *pieces,
        )

    arrived = [[] for _ in range(chunks)]
    for step in range(1, parts):
        ring = [(i, (i + 2 * step) % ctx_count) for i in range(ctx_count)]
        for c in range(chunks):
            piece = panel(step, c, grads[c], size * HD, BF16)
            arrived[c].append(sent(piece, ring))
    dk, dv = call(join_body, (shape((length, columns), BF16),) * 2, own, later)
    kept = panel(0, 0, sum(grads, []), columns, F32)
    held = []
    for c in range(chunks):
        held = [add(c * size * HD, kept, arrived[c], held)]
    return (dq[None], dk[None], dv[None], held[0][None])


def solution(mesh):
    rows = P("wide", "ctx", "head")
    return jax.shard_map(
        shards,
        mesh=mesh,
        in_specs=(rows, rows, rows, rows, P("wide", "ctx"), P(None, "ctx", "wide")),
        out_specs=(rows, rows, rows, rows),
        check_vma=False,
    )
```

```python
import functools

import jax
import jax.numpy as jnp
from jax import lax
from jax.experimental import pallas as pl
from jax.experimental.pallas import tpu as pltpu
from jax.sharding import PartitionSpec as P


HD = 128
F32 = jnp.float32
BF16 = jnp.bfloat16


def dot(left, right, left_dim, right_dim):
    return lax.dot_general(
        left, right, (((left_dim,), (right_dim,)), ((), ())), preferred_element_type=F32
    )


def vmem(dims, dtype):
    return pltpu.VMEM(dims, dtype)


def call(body, outs, *args, cost=1):
    whole = pl.BlockSpec(memory_space=pltpu.VMEM)
    args = [pltpu.with_memory_space_constraint(a, pltpu.VMEM) for a in args]
    return pl.pallas_call(
        body,
        out_shape=outs,
        in_specs=[whole] * len(args),
        out_specs=jax.tree.map(lambda _: whole, outs, is_leaf=lambda o: not isinstance(o, tuple)),
        cost_estimate=pl.CostEstimate(flops=cost << 20, bytes_accessed=1 << 20, transcendentals=0),
        compiler_params=pltpu.CompilerParams(vmem_limit_bytes=24 << 20),
    )(*args)


def shape(dims, dtype):
    return jax.ShapeDtypeStruct(dims, dtype)


def spread(row, length):
    part = jnp.transpose(jnp.broadcast_to(row.astype(F32), (HD, length)))
    return jnp.concatenate([part] * (length // HD), axis=1)


def head(h):
    return slice(h * HD, (h + 1) * HD)


def lower(length):
    rows = lax.broadcasted_iota(jnp.int32, (length, length), 0)
    return rows <= lax.broadcasted_iota(jnp.int32, (length, length), 1)


def masks(length, seg, pseg):
    own = lower(length)
    column = jnp.where(own, spread(seg[...], length), spread(pseg[...], length))
    return own, column == seg[...].astype(F32)


def head_prob(own, valid, qh, kh, pkh):
    scores = jnp.where(own, dot(kh, qh, 1, 1), dot(pkh, qh, 1, 1)) * HD ** (-0.5)
    scores = jnp.where(valid, scores, -jnp.inf)
    top = jnp.max(scores, axis=0, keepdims=True)
    weight = jnp.exp(scores - top)
    return weight * (1.0 / jnp.sum(weight, axis=0, keepdims=True))


def prob_body(length, heads, q, k, v, g, pk, seg, pseg, prob, own_grad):
    own, valid = masks(length, seg, pseg)
    for h in range(heads):
        at = head(h)
        prob[h] = head_prob(own, valid, q[:, at], k[:, at], pk[:, at])
        own_grad[h] = dot(v[:, at], g[:, at], 1, 1)


def query_body(length, heads, first, k, g, pk, pv, prob, own_grad, dq, ds):
    own = lower(length)
    own_query = jnp.logical_not(own) | (
        lax.broadcasted_iota(jnp.int32, (length, length), 0)
        == lax.broadcasted_iota(jnp.int32, (length, length), 1)
    )
    for h in range(heads):
        at = head(first + h)
        weight = prob[first + h]
        grad_prob = jnp.where(own, own_grad[first + h], dot(pv[:, at], g[:, at], 1, 1))
        grad_score = weight * (
            grad_prob - jnp.sum(weight * grad_prob, axis=0, keepdims=True)
        )
        ds[h] = grad_score
        turned = jnp.transpose(grad_score)
        own_part = jnp.where(own_query, turned, 0.0).astype(BF16)
        prior_part = jnp.where(own_query, 0.0, turned).astype(BF16)
        total = dot(own_part, k[:, at], 1, 0) + dot(prior_part, pk[:, at], 1, 0)
        dq[:, head(h)] = (total * HD ** (-0.5)).astype(BF16)


def terms_body(length, heads, size, q, g, prob, *refs):
    own_out, back_out, dq_out = refs[-3:]
    pieces = [refs[i : i + 2] for i in range(0, len(refs) - 3, 2)]
    own = lower(length)
    for c, (dq, _) in enumerate(pieces):
        dq_out[:, c * size * HD : (c + 1) * size * HD] = dq[...]
    for h in range(heads):
        at = head(h)
        ds = pieces[h // size][1]
        for index, (left, right) in enumerate(((ds[h % size], q), (prob[h], g))):
            own_out[index, :, at] = dot(
                jnp.where(own, left, 0.0).astype(BF16), right[:, at], 1, 0
            )
            back_out[index, :, at] = dot(
                jnp.where(own, 0.0, left).astype(BF16), right[:, at], 1, 0
            ).astype(BF16)


def join_body(own, later, dk, dv):
    dk[...] = ((own[0] + later[0].astype(F32)) * HD ** (-0.5)).astype(BF16)
    dv[...] = (own[1] + later[1].astype(F32)).astype(BF16)


def turn_body(recs, length, block, parts, frames, mine, theirs):
    for side in range(2):

        @pl.when(lax.rem(lax.axis_index("ctx"), 2) == side)
        def _():
            for part in range(parts):
                for r in range(recs):
                    for out, which in ((mine, side), (theirs, 1 - side)):
                        start = (2 * part + which) * block
                        tile = frames[r, :, start : start + block]
                        out[part, :, r * length : (r + 1) * length] = jnp.transpose(tile)


def panel_terms(count, length, step, frames, grads, ages):
    part = lax.rem(lax.div(lax.axis_index("ctx"), 2) + step, lax.axis_size("ctx") // 2)
    wide = lax.axis_index("wide")
    total = None
    for frame, grad, age in zip(frames, grads, ages):
        rec = lax.rem(wide - age + count, count)
        rows = pl.ds(pl.multiple_of(rec * length, HD), length)
        term = dot(frame[part, :, rows], grad, 1, 0)
        total = term if total is None else total + term
    return total


def first_body(count, length, step, chunk, mine_frames, peer_frames, mine, peer, *refs):
    came, out = refs[:-1], refs[-1]
    width = out.shape[1]
    at = slice(chunk * width, (chunk + 1) * width)
    out[...] = panel_terms(
        count, length, step,
        [mine_frames, peer_frames] + [mine_frames] * len(came),
        [mine[:, at], peer[:, at]] + [ref[...] for ref in came],
        [0, 0] + list(range(1, count)),
    )


def rest_body(count, length, step, peer_frames, begun, *refs):
    shared, out = refs[:-1], refs[-1]
    rest = panel_terms(
        count, length, step, [peer_frames] * len(shared), [ref[...] for ref in shared], range(1, count)
    )
    out[...] = (begun[...] + rest).astype(out.dtype)


def panel_body(count, length, mine_frames, peer_frames, mine, peer, *refs):
    grads, out = refs[:-1], refs[-1]
    each = 2 * (count - 1)
    width = out.shape[1] * each // len(grads)
    for c in range(out.shape[1] // width):
        at = slice(c * width, (c + 1) * width)
        mine_grads = [mine[:, at]] + [ref[...] for ref in grads[c * each : (c + 1) * each : 2]]
        peer_grads = [peer[:, at]] + [ref[...] for ref in grads[c * each + 1 : (c + 1) * each : 2]]
        out[:, at] = panel_terms(
            count, length, 0,
            [mine_frames] * count + [peer_frames] * count,
            mine_grads + peer_grads,
            list(range(count)) * 2,
        )


def add_body(first, *refs):
    refs, out = (refs[:-1] if first == 0 else refs[:-2]), refs[-1]
    total = refs[0][:, first : first + out.shape[1]]
    for ref in refs[1:]:
        total = total + ref[...].astype(F32)
    out[...] = total


def add(first, kept, arrived, held):
    whole = pl.BlockSpec(memory_space=pltpu.VMEM)
    rows, columns = arrived[0].shape
    args = [pltpu.with_memory_space_constraint(a, pltpu.VMEM) for a in (kept, *arrived)]
    return pl.pallas_call(
        functools.partial(add_body, first),
        grid=(1,),
        out_shape=shape(kept.shape, F32),
        in_specs=[whole] * len(args) + [pl.BlockSpec(memory_space=pl.ANY)] * len(held),
        out_specs=pl.BlockSpec((rows, columns), lambda i: (0, first // columns)),
        input_output_aliases={len(args): 0} if held else {},
        cost_estimate=pl.CostEstimate(flops=1 << 20, bytes_accessed=1 << 20, transcendentals=0),
        compiler_params=pltpu.CompilerParams(vmem_limit_bytes=24 << 20),
    )(*args, *held)


def shards(query_rows, key_rows, value_rows, grad_out, segment, frames):
    length, columns = query_rows.shape[1:]
    heads = columns // HD
    ctx_count = lax.axis_size("ctx")
    wide_count = lax.axis_size("wide")
    recs, _, width = frames.shape
    block = width // ctx_count
    parts = ctx_count // 2
    assert ctx_count >= 4 and recs == wide_count
    onward = [(i, (i + 1) % ctx_count) for i in range(ctx_count)]
    back = [(i, (i - 1) % ctx_count) for i in range(ctx_count)]
    other = [(i, i ^ 1) for i in range(ctx_count)]
    q, k, v, g = (a[0] for a in (query_rows, key_rows, value_rows, grad_out))

    def sent(value, pairs):
        return lax.ppermute(value, "ctx", pairs)

    pseg = sent(segment, onward)
    pk = sent(k, onward)
    pv = sent(v, onward)

    turned = vmem((parts, block, recs * length), BF16)
    mine, theirs = call(
        functools.partial(turn_body, recs, length, block, parts), (turned, turned), frames
    )
    given = lax.ppermute(theirs, "ctx", other)

    chunks = 2 if heads % 2 == 0 else 1
    size = heads // chunks
    square = vmem((heads, length, length), F32)
    prob, own_grad = call(
        functools.partial(prob_body, length, heads), (square, square),
        q, k, v, g, pk, segment, pseg,
    )
    found = []
    for c in range(chunks):
        found += call(
            functools.partial(query_body, length, size, c * size),
            (vmem((length, size * HD), BF16), vmem((size, length, length), F32)),
            k, g, pk, pv, prob, own_grad,
        )
    own, to_prior, dq = call(
        functools.partial(terms_body, length, heads, size),
        (
            vmem((2, length, columns), F32),
            vmem((2, length, columns), BF16),
            vmem((length, columns), BF16),
        ),
        q, g, prob, *found,
    )
    later = sent(to_prior, back)
    peer = sent(dq, other)
    grads = []
    for c in range(chunks):
        pieces = []
        for step in range(1, wide_count):
            ring = [(i, (i + step) % wide_count) for i in range(wide_count)]
            piece = lax.ppermute(found[2 * c], "wide", ring)
            pieces += [piece, sent(piece, other)]
        grads.append(pieces)

    arrived = [[] for _ in range(chunks)]
    for step in range(1, parts):
        ring = [(i, (i + 2 * step) % ctx_count) for i in range(ctx_count)]
        for c in range(chunks):
            begun = call(
                functools.partial(first_body, wide_count, length, step, c),
                vmem((block, size * HD), F32),
                mine, given, dq, peer, *grads[c][::2],
            )
            piece = call(
                functools.partial(rest_body, wide_count, length, step),
                vmem((block, size * HD), BF16),
                given, begun, *grads[c][1::2],
            )
            arrived[c].append(sent(piece, ring))
    dk, dv = call(join_body, (shape((length, columns), BF16),) * 2, own, later)
    kept = call(
        functools.partial(panel_body, wide_count, length),
        vmem((block, columns), F32),
        mine, given, dq, peer, *sum(grads, []),
    )
    held = []
    for c in range(chunks):
        held = [add(c * size * HD, kept, arrived[c], held)]
    return (dq[None], dk[None], dv[None], held[0][None])


def solution(mesh):
    rows = P("wide", "ctx", "head")
    return jax.shard_map(
        shards,
        mesh=mesh,
        in_specs=(rows, rows, rows, rows, P("wide", "ctx"), P(None, "ctx", "wide")),
        out_specs=(rows, rows, rows, rows),
        check_vma=False,
    )
```

```python
import functools

import jax
import jax.numpy as jnp
from jax import lax
from jax.experimental import pallas as pl
from jax.experimental.pallas import tpu as pltpu
from jax.sharding import PartitionSpec as P


HD = 128
F32 = jnp.float32
BF16 = jnp.bfloat16


def dot(left, right, left_dim, right_dim):
    return lax.dot_general(
        left, right, (((left_dim,), (right_dim,)), ((), ())), preferred_element_type=F32
    )


def vmem(dims, dtype):
    return pltpu.VMEM(dims, dtype)


def call(body, outs, *args, cost=1):
    whole = pl.BlockSpec(memory_space=pltpu.VMEM)
    args = [pltpu.with_memory_space_constraint(a, pltpu.VMEM) for a in args]
    return pl.pallas_call(
        body,
        out_shape=outs,
        in_specs=[whole] * len(args),
        out_specs=jax.tree.map(lambda _: whole, outs, is_leaf=lambda o: not isinstance(o, tuple)),
        cost_estimate=pl.CostEstimate(flops=cost << 20, bytes_accessed=1 << 20, transcendentals=0),
        compiler_params=pltpu.CompilerParams(vmem_limit_bytes=24 << 20),
    )(*args)


def shape(dims, dtype):
    return jax.ShapeDtypeStruct(dims, dtype)


def spread(row, length):
    part = jnp.transpose(jnp.broadcast_to(row.astype(F32), (HD, length)))
    return jnp.concatenate([part] * (length // HD), axis=1)


def head(h):
    return slice(h * HD, (h + 1) * HD)


def lower(length):
    rows = lax.broadcasted_iota(jnp.int32, (length, length), 0)
    return rows <= lax.broadcasted_iota(jnp.int32, (length, length), 1)


def masks(length, seg, pseg):
    own = lower(length)
    column = jnp.where(own, spread(seg[...], length), spread(pseg[...], length))
    return own, column == seg[...].astype(F32)


def head_prob(own, valid, qh, kh, pkh):
    scores = jnp.where(own, dot(kh, qh, 1, 1), dot(pkh, qh, 1, 1)) * HD ** (-0.5)
    scores = jnp.where(valid, scores, -jnp.inf)
    top = jnp.max(scores, axis=0, keepdims=True)
    weight = jnp.exp(scores - top)
    return weight * (1.0 / jnp.sum(weight, axis=0, keepdims=True))


def prob_body(length, heads, q, k, v, g, pk, seg, pseg, prob, turned, own_grad):
    own, valid = masks(length, seg, pseg)
    for h in range(heads):
        at = head(h)
        prob[h] = head_prob(own, valid, q[:, at], k[:, at], pk[:, at])
        turned[h] = jnp.transpose(prob[h])
        own_grad[h] = dot(g[:, at], v[:, at], 1, 1)


def upper(length):
    return lax.broadcasted_iota(jnp.int32, (length, length), 1) <= lax.broadcasted_iota(
        jnp.int32, (length, length), 0
    )


def query_body(length, heads, first, k, g, pk, pv, turned, own_grad, dq, ds):
    own = upper(length)
    step = length // 2
    blocks = [slice(start, start + step) for start in range(0, length, step)]
    for h in range(heads):
        at = head(first + h)
        weights = [turned[first + h, rows] for rows in blocks]
        grads = [
            jnp.where(own[rows], own_grad[first + h, rows], dot(g[rows, at], pv[:, at], 1, 1))
            for rows in blocks
        ]
        for rows, weight, grad_prob in zip(blocks, weights, grads):
            grad_score = weight * (
                grad_prob - jnp.sum(weight * grad_prob, axis=1, keepdims=True)
            )
            own_part = jnp.where(own[rows], grad_score, 0.0).astype(BF16)
            prior_part = jnp.where(own[rows], 0.0, grad_score).astype(BF16)
            total = dot(own_part, k[:, at], 1, 0) + dot(prior_part, pk[:, at], 1, 0)
            dq[rows, head(h)] = (total * HD ** (-0.5)).astype(BF16)
            ds[0, h, rows] = own_part
            ds[1, h, rows] = prior_part


def terms_body(length, heads, size, q, g, prob, *refs):
    own_out, back_out, dq_out = refs[-3:]
    pieces = [refs[i : i + 2] for i in range(0, len(refs) - 3, 2)]
    own = lower(length)
    for c, (dq, _) in enumerate(pieces):
        dq_out[:, c * size * HD : (c + 1) * size * HD] = dq[...]
    for h in range(heads):
        at = head(h)
        ds = pieces[h // size][1]
        own_out[0, :, at] = dot(ds[0, h % size], q[:, at], 0, 0)
        back_out[0, :, at] = dot(ds[1, h % size], q[:, at], 0, 0).astype(BF16)
        own_out[1, :, at] = dot(jnp.where(own, prob[h], 0.0).astype(BF16), g[:, at], 1, 0)
        back_out[1, :, at] = dot(
            jnp.where(own, 0.0, prob[h]).astype(BF16), g[:, at], 1, 0
        ).astype(BF16)


def join_body(own, later, dk, dv):
    dk[...] = ((own[0] + later[0].astype(F32)) * HD ** (-0.5)).astype(BF16)
    dv[...] = (own[1] + later[1].astype(F32)).astype(BF16)


def open_body(block, parts, *refs):
    count = (len(refs) - 6) // 2
    sources, frames = refs[:count], refs[count]
    outs, (mine, theirs) = refs[count + 1 : 2 * count + 1], refs[2 * count + 1 : 2 * count + 3]
    held, sems, frame_sems = refs[-3:]
    recs, length, _ = frames.shape
    copies = [
        pltpu.make_async_copy(source, out, sems.at[n]) for n, (source, out) in enumerate(zip(sources, outs))
    ]
    tiles = [(r, part) for part in range(parts) for r in range(recs)]
    loads = [
        pltpu.make_async_copy(
            frames.at[r, :, pl.ds(2 * part * block, 2 * block)], held.at[n], frame_sems.at[n]
        )
        for n, (r, part) in enumerate(tiles)
    ]
    for copy in loads + copies:
        copy.start()
    for n, (r, part) in enumerate(tiles):
        loads[n].wait()
        for side in range(2):

            @pl.when(lax.rem(lax.axis_index("ctx"), 2) == side)
            def _():
                for out, which in ((mine, side), (theirs, 1 - side)):
                    tile = held[n, :, which * block : (which + 1) * block]
                    out[part, :, r * length : (r + 1) * length] = jnp.transpose(tile)

    for copy in copies:
        copy.wait()


def open_all(parts, block, frames, *arrays):
    recs, length, _ = frames.shape
    outs = [vmem(a.shape, a.dtype) for a in arrays]
    outs += [vmem((parts, block, recs * length), BF16)] * 2
    return pl.pallas_call(
        functools.partial(open_body, block, parts),
        out_shape=tuple(outs),
        in_specs=[pl.BlockSpec(memory_space=pltpu.HBM)] * (len(arrays) + 1),
        out_specs=(pl.BlockSpec(memory_space=pltpu.VMEM),) * len(outs),
        scratch_shapes=[
            pltpu.VMEM((recs * parts, length, 2 * block), BF16),
            pltpu.SemaphoreType.DMA((len(arrays),)),
            pltpu.SemaphoreType.DMA((recs * parts,)),
        ],
        cost_estimate=pl.CostEstimate(flops=1 << 20, bytes_accessed=4 << 20, transcendentals=0),
        compiler_params=pltpu.CompilerParams(vmem_limit_bytes=24 << 20),
        name="open",
    )(*[pltpu.with_memory_space_constraint(a, pltpu.HBM) for a in (*arrays, frames)])


def panel_terms(count, length, step, frames, grads, ages):
    part = lax.rem(lax.div(lax.axis_index("ctx"), 2) + step, lax.axis_size("ctx") // 2)
    wide = lax.axis_index("wide")
    total = None
    for frame, grad, age in zip(frames, grads, ages):
        rec = lax.rem(wide - age + count, count)
        rows = pl.ds(pl.multiple_of(rec * length, HD), length)
        term = dot(frame[part, :, rows], grad, 1, 0)
        total = term if total is None else total + term
    return total


def first_body(count, length, step, chunk, mine_frames, peer_frames, mine, peer, *refs):
    came, out = refs[:-1], refs[-1]
    width = out.shape[1]
    at = slice(chunk * width, (chunk + 1) * width)
    out[...] = panel_terms(
        count, length, step,
        [mine_frames, peer_frames] + [mine_frames] * len(came),
        [mine[:, at], peer[:, at]] + [ref[...] for ref in came],
        [0, 0] + list(range(1, count)),
    )


def rest_body(count, length, step, peer_frames, begun, *refs):
    shared, out = refs[:-1], refs[-1]
    rest = panel_terms(
        count, length, step, [peer_frames] * len(shared), [ref[...] for ref in shared], range(1, count)
    )
    out[...] = (begun[...] + rest).astype(out.dtype)


def panel_body(count, length, mine_frames, peer_frames, mine, peer, *refs):
    grads, out = refs[:-1], refs[-1]
    each = 2 * (count - 1)
    width = out.shape[1] * each // len(grads)
    for c in range(out.shape[1] // width):
        at = slice(c * width, (c + 1) * width)
        mine_grads = [mine[:, at]] + [ref[...] for ref in grads[c * each : (c + 1) * each : 2]]
        peer_grads = [peer[:, at]] + [ref[...] for ref in grads[c * each + 1 : (c + 1) * each : 2]]
        out[:, at] = panel_terms(
            count, length, 0,
            [mine_frames] * count + [peer_frames] * count,
            mine_grads + peer_grads,
            list(range(count)) * 2,
        )


def add_body(first, *refs):
    refs, out = (refs[:-1] if first == 0 else refs[:-2]), refs[-1]
    total = refs[0][:, first : first + out.shape[1]]
    for ref in refs[1:]:
        total = total + ref[...].astype(F32)
    out[...] = total


def add(first, kept, arrived, held):
    whole = pl.BlockSpec(memory_space=pltpu.VMEM)
    rows, columns = arrived[0].shape
    args = [pltpu.with_memory_space_constraint(a, pltpu.VMEM) for a in (kept, *arrived)]
    return pl.pallas_call(
        functools.partial(add_body, first),
        grid=(1,),
        out_shape=shape(kept.shape, F32),
        in_specs=[whole] * len(args) + [pl.BlockSpec(memory_space=pl.ANY)] * len(held),
        out_specs=pl.BlockSpec((rows, columns), lambda i: (0, first // columns)),
        input_output_aliases={len(args): 0} if held else {},
        cost_estimate=pl.CostEstimate(flops=1 << 20, bytes_accessed=1 << 20, transcendentals=0),
        compiler_params=pltpu.CompilerParams(vmem_limit_bytes=24 << 20),
    )(*args, *held)


def shards(query_rows, key_rows, value_rows, grad_out, segment, frames):
    length, columns = query_rows.shape[1:]
    heads = columns // HD
    ctx_count = lax.axis_size("ctx")
    wide_count = lax.axis_size("wide")
    recs, _, width = frames.shape
    block = width // ctx_count
    parts = ctx_count // 2
    assert ctx_count >= 4 and recs == wide_count
    onward = [(i, (i + 1) % ctx_count) for i in range(ctx_count)]
    back = [(i, (i - 1) % ctx_count) for i in range(ctx_count)]
    other = [(i, i ^ 1) for i in range(ctx_count)]
    q, k, v, g = (a[0] for a in (query_rows, key_rows, value_rows, grad_out))

    def sent(value, pairs):
        return lax.ppermute(value, "ctx", pairs)

    pseg = sent(segment, onward)
    pk = sent(k, onward)
    pv = sent(v, onward)

    q, k, v, g, segment, mine, theirs = open_all(parts, block, frames, q, k, v, g, segment)
    given = lax.ppermute(theirs, "ctx", other)

    chunks = 2 if heads % 2 == 0 else 1
    size = heads // chunks
    square = vmem((heads, length, length), F32)
    prob, turned_prob, own_grad = call(
        functools.partial(prob_body, length, heads), (square, square, square),
        q, k, v, g, pk, segment, pseg,
    )
    found = []
    for c in range(chunks):
        found += call(
            functools.partial(query_body, length, size, c * size),
            (vmem((length, size * HD), BF16), vmem((2, size, length, length), BF16)),
            k, g, pk, pv, turned_prob, own_grad,
        )
    own, to_prior, dq = call(
        functools.partial(terms_body, length, heads, size),
        (
            vmem((2, length, columns), F32),
            vmem((2, length, columns), BF16),
            vmem((length, columns), BF16),
        ),
        q, g, prob, *found,
    )
    later = sent(to_prior, back)
    peer = sent(dq, other)
    grads = []
    for c in range(chunks):
        pieces = []
        for step in range(1, wide_count):
            ring = [(i, (i + step) % wide_count) for i in range(wide_count)]
            piece = lax.ppermute(found[2 * c], "wide", ring)
            pieces += [piece, sent(piece, other)]
        grads.append(pieces)

    arrived = [[] for _ in range(chunks)]
    for step in range(1, parts):
        ring = [(i, (i + 2 * step) % ctx_count) for i in range(ctx_count)]
        for c in range(chunks):
            begun = call(
                functools.partial(first_body, wide_count, length, step, c),
                vmem((block, size * HD), F32),
                mine, given, dq, peer, *grads[c][::2],
            )
            piece = call(
                functools.partial(rest_body, wide_count, length, step),
                vmem((block, size * HD), BF16),
                given, begun, *grads[c][1::2],
            )
            arrived[c].append(sent(piece, ring))
    dk, dv = call(join_body, (shape((length, columns), BF16),) * 2, own, later)
    kept = call(
        functools.partial(panel_body, wide_count, length),
        vmem((block, columns), F32),
        mine, given, dq, peer, *sum(grads, []),
    )
    held = []
    for c in range(chunks):
        held = [add(c * size * HD, kept, arrived[c], held)]
    return (dq[None], dk[None], dv[None], held[0][None])


def solution(mesh):
    rows = P("wide", "ctx", "head")
    return jax.shard_map(
        shards,
        mesh=mesh,
        in_specs=(rows, rows, rows, rows, P("wide", "ctx"), P(None, "ctx", "wide")),
        out_specs=(rows, rows, rows, rows),
        check_vma=False,
    )
```

```python
import functools

import jax
import jax.numpy as jnp
from jax import lax
from jax.experimental import pallas as pl
from jax.experimental.pallas import tpu as pltpu
from jax.sharding import PartitionSpec as P


HD = 128
F32 = jnp.float32
BF16 = jnp.bfloat16


def dot(left, right, left_dim, right_dim):
    return lax.dot_general(
        left, right, (((left_dim,), (right_dim,)), ((), ())), preferred_element_type=F32
    )


def vmem(dims, dtype):
    return pltpu.VMEM(dims, dtype)


def call(body, outs, *args, cost=1):
    whole = pl.BlockSpec(memory_space=pltpu.VMEM)
    args = [pltpu.with_memory_space_constraint(a, pltpu.VMEM) for a in args]
    return pl.pallas_call(
        body,
        out_shape=outs,
        in_specs=[whole] * len(args),
        out_specs=jax.tree.map(lambda _: whole, outs, is_leaf=lambda o: not isinstance(o, tuple)),
        cost_estimate=pl.CostEstimate(flops=cost << 20, bytes_accessed=1 << 20, transcendentals=0),
        compiler_params=pltpu.CompilerParams(vmem_limit_bytes=24 << 20),
    )(*args)


def shape(dims, dtype):
    return jax.ShapeDtypeStruct(dims, dtype)


def spread(row, length):
    part = jnp.transpose(jnp.broadcast_to(row.astype(F32), (HD, length)))
    return jnp.concatenate([part] * (length // HD), axis=1)


def head(h):
    return slice(h * HD, (h + 1) * HD)


def lower(length):
    rows = lax.broadcasted_iota(jnp.int32, (length, length), 0)
    return rows <= lax.broadcasted_iota(jnp.int32, (length, length), 1)


def masks(length, seg, pseg):
    own = lower(length)
    column = jnp.where(own, spread(seg[...], length), spread(pseg[...], length))
    return own, column == seg[...].astype(F32)


def head_prob(own, valid, qh, kh, pkh):
    scores = jnp.where(own, dot(kh, qh, 1, 1), dot(pkh, qh, 1, 1)) * HD ** (-0.5)
    scores = jnp.where(valid, scores, -jnp.inf)
    top = jnp.max(scores, axis=0, keepdims=True)
    weight = jnp.exp(scores - top)
    return weight * (1.0 / jnp.sum(weight, axis=0, keepdims=True))


def prob_body(length, heads, q, k, v, g, pk, seg, pseg, prob, turned, own_grad):
    own, valid = masks(length, seg, pseg)
    for h in range(heads):
        at = head(h)
        prob[h] = head_prob(own, valid, q[:, at], k[:, at], pk[:, at])
        turned[h] = jnp.transpose(prob[h])
        own_grad[h] = dot(g[:, at], v[:, at], 1, 1)


def upper(length):
    return lax.broadcasted_iota(jnp.int32, (length, length), 1) <= lax.broadcasted_iota(
        jnp.int32, (length, length), 0
    )


def query_body(length, heads, first, k, g, pk, pv, turned, own_grad, dq, ds):
    own = upper(length)
    step = length // 2
    blocks = [slice(start, start + step) for start in range(0, length, step)]
    for h in range(heads):
        at = head(first + h)
        weights = [turned[first + h, rows] for rows in blocks]
        grads = [
            jnp.where(own[rows], own_grad[first + h, rows], dot(g[rows, at], pv[:, at], 1, 1))
            for rows in blocks
        ]
        for rows, weight, grad_prob in zip(blocks, weights, grads):
            grad_score = weight * (
                grad_prob - jnp.sum(weight * grad_prob, axis=1, keepdims=True)
            )
            own_part = jnp.where(own[rows], grad_score, 0.0).astype(BF16)
            prior_part = jnp.where(own[rows], 0.0, grad_score).astype(BF16)
            total = dot(own_part, k[:, at], 1, 0) + dot(prior_part, pk[:, at], 1, 0)
            dq[rows, head(h)] = (total * HD ** (-0.5)).astype(BF16)
            ds[0, h, rows] = own_part
            ds[1, h, rows] = prior_part


def values_body(length, heads, g, prob, own_out, back_out):
    own = lower(length)
    for h in range(heads):
        at = head(h)
        own_out[:, at] = dot(jnp.where(own, prob[h], 0.0).astype(BF16), g[:, at], 1, 0)
        back_out[:, at] = dot(
            jnp.where(own, 0.0, prob[h]).astype(BF16), g[:, at], 1, 0
        ).astype(BF16)


def keys_body(heads, size, q, *refs):
    own_out, back_out, dq_out = refs[-3:]
    pieces = [refs[i : i + 2] for i in range(0, len(refs) - 3, 2)]
    for c, (dq, _) in enumerate(pieces):
        dq_out[:, c * size * HD : (c + 1) * size * HD] = dq[...]
    for h in range(heads):
        at = head(h)
        ds = pieces[h // size][1]
        own_out[:, at] = dot(ds[0, h % size], q[:, at], 0, 0)
        back_out[:, at] = dot(ds[1, h % size], q[:, at], 0, 0).astype(BF16)


def join_body(own_key, later_key, own_value, later_value, dk, dv):
    dk[...] = ((own_key[...] + later_key[...].astype(F32)) * HD ** (-0.5)).astype(BF16)
    dv[...] = (own_value[...] + later_value[...].astype(F32)).astype(BF16)


def open_body(block, parts, *refs):
    count = (len(refs) - 6) // 2
    sources, frames = refs[:count], refs[count]
    outs, (mine, theirs) = refs[count + 1 : 2 * count + 1], refs[2 * count + 1 : 2 * count + 3]
    held, sems, frame_sems = refs[-3:]
    recs, length, _ = frames.shape
    copies = [
        pltpu.make_async_copy(source, out, sems.at[n]) for n, (source, out) in enumerate(zip(sources, outs))
    ]
    tiles = [(r, part) for part in range(parts) for r in range(recs)]
    loads = [
        pltpu.make_async_copy(
            frames.at[r, :, pl.ds(2 * part * block, 2 * block)], held.at[n], frame_sems.at[n]
        )
        for n, (r, part) in enumerate(tiles)
    ]
    for copy in loads + copies:
        copy.start()
    for n, (r, part) in enumerate(tiles):
        loads[n].wait()
        for side in range(2):

            @pl.when(lax.rem(lax.axis_index("ctx"), 2) == side)
            def _():
                for out, which in ((mine, side), (theirs, 1 - side)):
                    tile = held[n, :, which * block : (which + 1) * block]
                    out[part, :, r * length : (r + 1) * length] = jnp.transpose(tile)

    for copy in copies:
        copy.wait()


def open_all(parts, block, frames, *arrays):
    recs, length, _ = frames.shape
    outs = [vmem(a.shape, a.dtype) for a in arrays]
    outs += [vmem((parts, block, recs * length), BF16)] * 2
    return pl.pallas_call(
        functools.partial(open_body, block, parts),
        out_shape=tuple(outs),
        in_specs=[pl.BlockSpec(memory_space=pltpu.HBM)] * (len(arrays) + 1),
        out_specs=(pl.BlockSpec(memory_space=pltpu.VMEM),) * len(outs),
        scratch_shapes=[
            pltpu.VMEM((recs * parts, length, 2 * block), BF16),
            pltpu.SemaphoreType.DMA((len(arrays),)),
            pltpu.SemaphoreType.DMA((recs * parts,)),
        ],
        cost_estimate=pl.CostEstimate(flops=1 << 20, bytes_accessed=4 << 20, transcendentals=0),
        compiler_params=pltpu.CompilerParams(vmem_limit_bytes=24 << 20),
        name="open",
    )(*[pltpu.with_memory_space_constraint(a, pltpu.HBM) for a in (*arrays, frames)])


def panel_terms(count, length, step, frames, grads, ages):
    part = lax.rem(lax.div(lax.axis_index("ctx"), 2) + step, lax.axis_size("ctx") // 2)
    wide = lax.axis_index("wide")
    total = None
    for frame, grad, age in zip(frames, grads, ages):
        rec = lax.rem(wide - age + count, count)
        rows = pl.ds(pl.multiple_of(rec * length, HD), length)
        term = dot(frame[part, :, rows], grad, 1, 0)
        total = term if total is None else total + term
    return total


def first_body(count, length, step, chunk, mine_frames, peer_frames, mine, peer, *refs):
    came, out = refs[:-1], refs[-1]
    width = out.shape[1]
    at = slice(chunk * width, (chunk + 1) * width)
    out[...] = panel_terms(
        count, length, step,
        [mine_frames, peer_frames] + [mine_frames] * len(came),
        [mine[:, at], peer[:, at]] + [ref[...] for ref in came],
        [0, 0] + list(range(1, count)),
    )


def rest_body(count, length, step, peer_frames, begun, *refs):
    shared, out = refs[:-1], refs[-1]
    rest = panel_terms(
        count, length, step, [peer_frames] * len(shared), [ref[...] for ref in shared], range(1, count)
    )
    out[...] = (begun[...] + rest).astype(out.dtype)


def panel_body(count, length, mine_frames, peer_frames, mine, peer, *refs):
    grads, out = refs[:-1], refs[-1]
    each = 2 * (count - 1)
    width = out.shape[1] * each // len(grads)
    for c in range(out.shape[1] // width):
        at = slice(c * width, (c + 1) * width)
        mine_grads = [mine[:, at]] + [ref[...] for ref in grads[c * each : (c + 1) * each : 2]]
        peer_grads = [peer[:, at]] + [ref[...] for ref in grads[c * each + 1 : (c + 1) * each : 2]]
        out[:, at] = panel_terms(
            count, length, 0,
            [mine_frames] * count + [peer_frames] * count,
            mine_grads + peer_grads,
            list(range(count)) * 2,
        )


def add_body(first, *refs):
    refs, out = (refs[:-1] if first == 0 else refs[:-2]), refs[-1]
    total = refs[0][:, first : first + out.shape[1]]
    for ref in refs[1:]:
        total = total + ref[...].astype(F32)
    out[...] = total


def add(first, kept, arrived, held):
    whole = pl.BlockSpec(memory_space=pltpu.VMEM)
    rows, columns = arrived[0].shape
    args = [pltpu.with_memory_space_constraint(a, pltpu.VMEM) for a in (kept, *arrived)]
    return pl.pallas_call(
        functools.partial(add_body, first),
        grid=(1,),
        out_shape=shape(kept.shape, F32),
        in_specs=[whole] * len(args) + [pl.BlockSpec(memory_space=pl.ANY)] * len(held),
        out_specs=pl.BlockSpec((rows, columns), lambda i: (0, first // columns)),
        input_output_aliases={len(args): 0} if held else {},
        cost_estimate=pl.CostEstimate(flops=1 << 20, bytes_accessed=1 << 20, transcendentals=0),
        compiler_params=pltpu.CompilerParams(vmem_limit_bytes=24 << 20),
    )(*args, *held)


def shards(query_rows, key_rows, value_rows, grad_out, segment, frames):
    length, columns = query_rows.shape[1:]
    heads = columns // HD
    ctx_count = lax.axis_size("ctx")
    wide_count = lax.axis_size("wide")
    recs, _, width = frames.shape
    block = width // ctx_count
    parts = ctx_count // 2
    assert ctx_count >= 4 and recs == wide_count
    onward = [(i, (i + 1) % ctx_count) for i in range(ctx_count)]
    back = [(i, (i - 1) % ctx_count) for i in range(ctx_count)]
    other = [(i, i ^ 1) for i in range(ctx_count)]
    q, k, v, g = (a[0] for a in (query_rows, key_rows, value_rows, grad_out))

    def sent(value, pairs):
        return lax.ppermute(value, "ctx", pairs)

    pseg = sent(segment, onward)
    pk = sent(k, onward)
    pv = sent(v, onward)

    q, k, v, g, segment, mine, theirs = open_all(parts, block, frames, q, k, v, g, segment)
    given = lax.ppermute(theirs, "ctx", other)

    chunks = 2 if heads % 2 == 0 else 1
    size = heads // chunks
    square = vmem((heads, length, length), F32)
    prob, turned_prob, own_grad = call(
        functools.partial(prob_body, length, heads), (square, square, square),
        q, k, v, g, pk, segment, pseg,
    )
    sums = (vmem((length, columns), F32), vmem((length, columns), BF16))
    own_value, back_value = call(functools.partial(values_body, length, heads), sums, g, prob)
    later_value = sent(back_value, back)
    found = []
    for c in range(chunks):
        found += call(
            functools.partial(query_body, length, size, c * size),
            (vmem((length, size * HD), BF16), vmem((2, size, length, length), BF16)),
            k, g, pk, pv, turned_prob, own_grad,
        )
    own_key, back_key, dq = call(
        functools.partial(keys_body, heads, size),
        (*sums, vmem((length, columns), BF16)),
        q, *found,
    )
    later_key = sent(back_key, back)
    peer = sent(dq, other)
    grads = []
    for c in range(chunks):
        pieces = []
        for step in range(1, wide_count):
            ring = [(i, (i + step) % wide_count) for i in range(wide_count)]
            piece = lax.ppermute(found[2 * c], "wide", ring)
            pieces += [piece, sent(piece, other)]
        grads.append(pieces)

    arrived = [[] for _ in range(chunks)]
    for step in range(1, parts):
        ring = [(i, (i + 2 * step) % ctx_count) for i in range(ctx_count)]
        for c in range(chunks):
            begun = call(
                functools.partial(first_body, wide_count, length, step, c),
                vmem((block, size * HD), F32),
                mine, given, dq, peer, *grads[c][::2],
            )
            piece = call(
                functools.partial(rest_body, wide_count, length, step),
                vmem((block, size * HD), BF16),
                given, begun, *grads[c][1::2],
            )
            arrived[c].append(sent(piece, ring))
    dk, dv = call(join_body, (shape((length, columns), BF16),) * 2, own_key, later_key, own_value, later_value)
    kept = call(
        functools.partial(panel_body, wide_count, length),
        vmem((block, columns), F32),
        mine, given, dq, peer, *sum(grads, []),
    )
    held = []
    for c in range(chunks):
        held = [add(c * size * HD, kept, arrived[c], held)]
    return (dq[None], dk[None], dv[None], held[0][None])


def solution(mesh):
    rows = P("wide", "ctx", "head")
    return jax.shard_map(
        shards,
        mesh=mesh,
        in_specs=(rows, rows, rows, rows, P("wide", "ctx"), P(None, "ctx", "wide")),
        out_specs=(rows, rows, rows, rows),
        check_vma=False,
    )
```

```python
import functools

import jax
import jax.numpy as jnp
from jax import lax
from jax.experimental import pallas as pl
from jax.experimental.pallas import tpu as pltpu
from jax.sharding import PartitionSpec as P


HD = 128
F32 = jnp.float32
BF16 = jnp.bfloat16


def dot(left, right, left_dim, right_dim):
    return lax.dot_general(
        left, right, (((left_dim,), (right_dim,)), ((), ())), preferred_element_type=F32
    )


def vmem(dims, dtype):
    return pltpu.VMEM(dims, dtype)


def call(body, outs, *args, cost=1):
    whole = pl.BlockSpec(memory_space=pltpu.VMEM)
    args = [pltpu.with_memory_space_constraint(a, pltpu.VMEM) for a in args]
    return pl.pallas_call(
        body,
        out_shape=outs,
        in_specs=[whole] * len(args),
        out_specs=jax.tree.map(lambda _: whole, outs, is_leaf=lambda o: not isinstance(o, tuple)),
        cost_estimate=pl.CostEstimate(flops=cost << 20, bytes_accessed=1 << 20, transcendentals=0),
        compiler_params=pltpu.CompilerParams(vmem_limit_bytes=24 << 20),
    )(*args)


def shape(dims, dtype):
    return jax.ShapeDtypeStruct(dims, dtype)


def spread(row, length):
    part = jnp.transpose(jnp.broadcast_to(row.astype(F32), (HD, length)))
    return jnp.concatenate([part] * (length // HD), axis=1)


def head(h):
    return slice(h * HD, (h + 1) * HD)


def lower(length):
    rows = lax.broadcasted_iota(jnp.int32, (length, length), 0)
    return rows <= lax.broadcasted_iota(jnp.int32, (length, length), 1)


def masks(length, seg, pseg):
    own = lower(length)
    column = jnp.where(own, spread(seg[...], length), spread(pseg[...], length))
    return own, column == seg[...].astype(F32)


def head_prob(own, valid, qh, kh, pkh):
    scores = jnp.where(own, dot(kh, qh, 1, 1), dot(pkh, qh, 1, 1)) * HD ** (-0.5)
    scores = jnp.where(valid, scores, -jnp.inf)
    top = jnp.max(scores, axis=0, keepdims=True)
    weight = jnp.exp(scores - top)
    return weight * (1.0 / jnp.sum(weight, axis=0, keepdims=True))


def prob_body(length, heads, q, k, v, g, pk, seg, pseg, prob, turned, own_grad):
    own, valid = masks(length, seg, pseg)
    for h in range(heads):
        at = head(h)
        prob[h] = head_prob(own, valid, q[:, at], k[:, at], pk[:, at])
        turned[h] = jnp.transpose(prob[h])
        own_grad[h] = dot(g[:, at], v[:, at], 1, 1)


def upper(length):
    return lax.broadcasted_iota(jnp.int32, (length, length), 1) <= lax.broadcasted_iota(
        jnp.int32, (length, length), 0
    )


def query_body(length, heads, first, k, g, pk, pv, turned, own_grad, dq, ds):
    own = upper(length)
    step = length // 2
    blocks = [slice(start, start + step) for start in range(0, length, step)]
    for h in range(heads):
        at = head(first + h)
        weights = [turned[first + h, rows] for rows in blocks]
        grads = [
            jnp.where(own[rows], own_grad[first + h, rows], dot(g[rows, at], pv[:, at], 1, 1))
            for rows in blocks
        ]
        for rows, weight, grad_prob in zip(blocks, weights, grads):
            grad_score = weight * (
                grad_prob - jnp.sum(weight * grad_prob, axis=1, keepdims=True)
            )
            own_part = jnp.where(own[rows], grad_score, 0.0).astype(BF16)
            prior_part = jnp.where(own[rows], 0.0, grad_score).astype(BF16)
            total = dot(own_part, k[:, at], 1, 0) + dot(prior_part, pk[:, at], 1, 0)
            dq[rows, head(h)] = (total * HD ** (-0.5)).astype(BF16)
            ds[0, h, rows] = own_part
            ds[1, h, rows] = prior_part


def values_body(length, heads, g, prob, own_out, back_out):
    own = lower(length)
    for h in range(heads):
        at = head(h)
        own_out[:, at] = dot(jnp.where(own, prob[h], 0.0).astype(BF16), g[:, at], 1, 0)
        back_out[:, at] = dot(
            jnp.where(own, 0.0, prob[h]).astype(BF16), g[:, at], 1, 0
        ).astype(BF16)


def keys_body(heads, size, q, *refs):
    own_out, back_out, dq_out = refs[-3:]
    pieces = [refs[i : i + 2] for i in range(0, len(refs) - 3, 2)]
    for c, (dq, _) in enumerate(pieces):
        dq_out[:, c * size * HD : (c + 1) * size * HD] = dq[...]
    for h in range(heads):
        at = head(h)
        ds = pieces[h // size][1]
        own_out[:, at] = dot(ds[0, h % size], q[:, at], 0, 0)
        back_out[:, at] = dot(ds[1, h % size], q[:, at], 0, 0).astype(BF16)


def join_body(own_key, later_key, own_value, later_value, dk, dv):
    dk[...] = ((own_key[...] + later_key[...].astype(F32)) * HD ** (-0.5)).astype(BF16)
    dv[...] = (own_value[...] + later_value[...].astype(F32)).astype(BF16)


def open_body(block, parts, *refs):
    count = (len(refs) - 6) // 2
    sources, frames = refs[:count], refs[count]
    outs, (mine, theirs) = refs[count + 1 : 2 * count + 1], refs[2 * count + 1 : 2 * count + 3]
    held, sems, frame_sems = refs[-3:]
    recs, length, _ = frames.shape
    copies = [
        pltpu.make_async_copy(source, out, sems.at[n]) for n, (source, out) in enumerate(zip(sources, outs))
    ]
    tiles = [(r, part) for part in range(parts) for r in range(recs)]
    loads = [
        pltpu.make_async_copy(
            frames.at[r, :, pl.ds(2 * part * block, 2 * block)], held.at[n], frame_sems.at[n]
        )
        for n, (r, part) in enumerate(tiles)
    ]
    for copy in loads + copies:
        copy.start()
    for n, (r, part) in enumerate(tiles):
        loads[n].wait()
        for side in range(2):

            @pl.when(lax.rem(lax.axis_index("ctx"), 2) == side)
            def _():
                for out, which in ((mine, side), (theirs, 1 - side)):
                    tile = held[n, :, which * block : (which + 1) * block]
                    out[part, :, r * length : (r + 1) * length] = jnp.transpose(tile)

    for copy in copies:
        copy.wait()


def open_all(parts, block, frames, *arrays):
    recs, length, _ = frames.shape
    outs = [vmem(a.shape, a.dtype) for a in arrays]
    outs += [vmem((parts, block, recs * length), BF16)] * 2
    return pl.pallas_call(
        functools.partial(open_body, block, parts),
        out_shape=tuple(outs),
        in_specs=[pl.BlockSpec(memory_space=pltpu.HBM)] * (len(arrays) + 1),
        out_specs=(pl.BlockSpec(memory_space=pltpu.VMEM),) * len(outs),
        scratch_shapes=[
            pltpu.VMEM((recs * parts, length, 2 * block), BF16),
            pltpu.SemaphoreType.DMA((len(arrays),)),
            pltpu.SemaphoreType.DMA((recs * parts,)),
        ],
        cost_estimate=pl.CostEstimate(flops=1 << 20, bytes_accessed=4 << 20, transcendentals=0),
        compiler_params=pltpu.CompilerParams(vmem_limit_bytes=24 << 20),
        name="open",
    )(*[pltpu.with_memory_space_constraint(a, pltpu.HBM) for a in (*arrays, frames)])


def panel_terms(count, length, step, frames, grads, ages):
    part = lax.rem(lax.div(lax.axis_index("ctx"), 2) + step, lax.axis_size("ctx") // 2)
    wide = lax.axis_index("wide")
    total = None
    for frame, grad, age in zip(frames, grads, ages):
        rec = lax.rem(wide - age + count, count)
        rows = pl.ds(pl.multiple_of(rec * length, HD), length)
        term = dot(frame[part, :, rows], grad, 1, 0)
        total = term if total is None else total + term
    return total


def first_body(count, length, step, chunk, mine_frames, peer_frames, mine, peer, *refs):
    came, out = refs[:-1], refs[-1]
    width = out.shape[1]
    at = slice(chunk * width, (chunk + 1) * width)
    out[...] = panel_terms(
        count, length, step,
        [mine_frames, peer_frames] + [mine_frames] * len(came),
        [mine[:, at], peer[:, at]] + [ref[...] for ref in came],
        [0, 0] + list(range(1, count)),
    )


def rest_body(count, length, step, peer_frames, begun, *refs):
    shared, out = refs[:-1], refs[-1]
    rest = panel_terms(
        count, length, step, [peer_frames] * len(shared), [ref[...] for ref in shared], range(1, count)
    )
    out[...] = (begun[...] + rest).astype(out.dtype)


def panel_body(count, length, mine_frames, peer_frames, mine, peer, *refs):
    grads, out = refs[:-1], refs[-1]
    each = 2 * (count - 1)
    width = out.shape[1] * each // len(grads)
    for c in range(out.shape[1] // width):
        at = slice(c * width, (c + 1) * width)
        mine_grads = [mine[:, at]] + [ref[...] for ref in grads[c * each : (c + 1) * each : 2]]
        peer_grads = [peer[:, at]] + [ref[...] for ref in grads[c * each + 1 : (c + 1) * each : 2]]
        out[:, at] = panel_terms(
            count, length, 0,
            [mine_frames] * count + [peer_frames] * count,
            mine_grads + peer_grads,
            list(range(count)) * 2,
        )


def add_body(first, *refs):
    refs, out = (refs[:-1] if first == 0 else refs[:-2]), refs[-1]
    size = out.shape[0]
    rows = pl.ds(pl.multiple_of(pl.program_id(0) * size, 8), size)
    total = refs[0][rows, first : first + out.shape[1]]
    for ref in refs[1:]:
        total = total + ref[rows].astype(F32)
    out[...] = total


def add(first, kept, arrived, held):
    whole = pl.BlockSpec(memory_space=pltpu.VMEM)
    rows, columns = arrived[0].shape
    args = [pltpu.with_memory_space_constraint(a, pltpu.VMEM) for a in (kept, *arrived)]
    return pl.pallas_call(
        functools.partial(add_body, first),
        grid=(2,),
        out_shape=shape(kept.shape, F32),
        in_specs=[whole] * len(args) + [pl.BlockSpec(memory_space=pl.ANY)] * len(held),
        out_specs=pl.BlockSpec((rows // 2, columns), lambda i: (i, first // columns)),
        input_output_aliases={len(args): 0} if held else {},
        cost_estimate=pl.CostEstimate(flops=1 << 20, bytes_accessed=1 << 20, transcendentals=0),
        compiler_params=pltpu.CompilerParams(vmem_limit_bytes=24 << 20),
    )(*args, *held)


def shards(query_rows, key_rows, value_rows, grad_out, segment, frames):
    length, columns = query_rows.shape[1:]
    heads = columns // HD
    ctx_count = lax.axis_size("ctx")
    wide_count = lax.axis_size("wide")
    recs, _, width = frames.shape
    block = width // ctx_count
    parts = ctx_count // 2
    assert ctx_count >= 4 and recs == wide_count
    onward = [(i, (i + 1) % ctx_count) for i in range(ctx_count)]
    back = [(i, (i - 1) % ctx_count) for i in range(ctx_count)]
    other = [(i, i ^ 1) for i in range(ctx_count)]
    q, k, v, g = (a[0] for a in (query_rows, key_rows, value_rows, grad_out))

    def sent(value, pairs):
        return lax.ppermute(value, "ctx", pairs)

    pseg = sent(segment, onward)
    pk = sent(k, onward)
    pv = sent(v, onward)

    q, k, v, g, segment, mine, theirs = open_all(parts, block, frames, q, k, v, g, segment)
    given = lax.ppermute(theirs, "ctx", other)

    chunks = 2 if heads % 2 == 0 else 1
    size = heads // chunks
    square = vmem((heads, length, length), F32)
    prob, turned_prob, own_grad = call(
        functools.partial(prob_body, length, heads), (square, square, square),
        q, k, v, g, pk, segment, pseg,
    )
    sums = (vmem((length, columns), F32), vmem((length, columns), BF16))
    own_value, back_value = call(functools.partial(values_body, length, heads), sums, g, prob)
    later_value = sent(back_value, back)
    found = []
    for c in range(chunks):
        found += call(
            functools.partial(query_body, length, size, c * size),
            (vmem((length, size * HD), BF16), vmem((2, size, length, length), BF16)),
            k, g, pk, pv, turned_prob, own_grad,
        )
    own_key, back_key, dq = call(
        functools.partial(keys_body, heads, size),
        (*sums, vmem((length, columns), BF16)),
        q, *found,
    )
    later_key = sent(back_key, back)
    peer = sent(dq, other)
    grads = []
    for c in range(chunks):
        pieces = []
        for step in range(1, wide_count):
            ring = [(i, (i + step) % wide_count) for i in range(wide_count)]
            piece = lax.ppermute(found[2 * c], "wide", ring)
            pieces += [piece, sent(piece, other)]
        grads.append(pieces)

    arrived = [[] for _ in range(chunks)]
    for step in range(1, parts):
        ring = [(i, (i + 2 * step) % ctx_count) for i in range(ctx_count)]
        for c in range(chunks):
            begun = call(
                functools.partial(first_body, wide_count, length, step, c),
                vmem((block, size * HD), F32),
                mine, given, dq, peer, *grads[c][::2],
            )
            piece = call(
                functools.partial(rest_body, wide_count, length, step),
                vmem((block, size * HD), BF16),
                given, begun, *grads[c][1::2],
            )
            arrived[c].append(sent(piece, ring))
    dk, dv = call(join_body, (shape((length, columns), BF16),) * 2, own_key, later_key, own_value, later_value)
    kept = call(
        functools.partial(panel_body, wide_count, length),
        vmem((block, columns), F32),
        mine, given, dq, peer, *sum(grads, []),
    )
    held = []
    for c in range(chunks):
        held = [add(c * size * HD, kept, arrived[c], held)]
    return (dq[None], dk[None], dv[None], held[0][None])


def solution(mesh):
    rows = P("wide", "ctx", "head")
    return jax.shard_map(
        shards,
        mesh=mesh,
        in_specs=(rows, rows, rows, rows, P("wide", "ctx"), P(None, "ctx", "wide")),
        out_specs=(rows, rows, rows, rows),
        check_vma=False,
    )
```
